256 devices in a mesh: pipe: 2 (over core), tensor: 32 (over z, x), dp: 4 (over y).
Axes of the slice: x: 4, y: 4, z: 8, core: 2. Of those that a mesh axis runs over, the one named last changes fastest.
Arguments:
- cotangent: bfloat16 [2, 2048, 8192], P(None, 'dp', 'tensor'), may hold values from -6 to 6
- saved_short: bfloat16 [2, 2, 2048, 8192], P('pipe', None, 'dp', 'tensor'), may hold values from -3.5 to 3.5
- saved_medium: bfloat16 [2, 2, 2048, 8192], P('pipe', None, 'dp', 'tensor'), may hold values from -3.5 to 3.5
- out_weight: bfloat16 [2, 8192, 8192], P('pipe', 'tensor'), may hold values from -0.0625 to 0.0625
- short_filter: float32 [2, 7, 8192], P('pipe', None, 'tensor'), may hold values from -2.5 to 2.5
- medium_filter: float32 [2, 128, 8192], P('pipe', None, 'tensor'), may hold values from -0.5 to 0.5
- proj_in: bfloat16 [2, 8192, 64], P('pipe', 'tensor'), may hold values from -0.0625 to 0.0625
- proj_out: bfloat16 [2, 8192, 64], P('pipe'), may hold values from -0.0625 to 0.0625
Outputs:
- proj_grads: float32 [2, 2, 64, 64], P('pipe')
The draws below stay inside these ranges and needn't reach their ends.
All inputs are finite; a program needn't handle non-finite values.
Results may differ from the reference program's by a relative error of at most 0.0041.
Values may be sent and summed in bfloat16 or wider, within the bound.
No kernel may reach another device: no remote copies, remote signals or barrier semaphores. Data moves between devices by JAX's collectives and lax.ppermute only.
A program may use at most 128 MiB of HBM per device.

```python
import math
import jax
import jax.numpy as jnp
from jax import lax

D = 8192
RANK = 64
SHORT_TAPS = 7
MED_TAPS = 128
MICRO = 2
LAYERS = 2
SEQ = 2048


def steps_of(key, shape, cuts, least, high):
    def one(dim, shards_of):
        draws = jax.random.uniform(jax.random.fold_in(jax.random.fold_in(key, 6), dim), (shards_of,), jnp.float32, least / len(cuts), high / len(cuts))
        return jnp.repeat(jnp.exp(draws), shape[dim] // shards_of).reshape((-1,) + (1,) * (len(shape) - dim - 1))

    level = one(*cuts[0])
    for cut in cuts[1:]:
        level = level * one(*cut)
    return level


def centred(own_key, dims, scale, most, split=(), kind=jnp.bfloat16):
    values = jax.random.normal(own_key, dims, jnp.float32) * scale
    if len(split) > 0:
        values = steps_of(own_key, dims, split, -0.22, 0.18) * values
    return jnp.clip(values, min=-most, max=most).astype(kind)


def setup_inputs(seed: int = 0) -> dict:
    seeds = jax.random.split(jax.random.key(seed), 9)
    return {
        "cotangent": centred(seeds[0], (MICRO, SEQ, D), 1.0, 6.0, ((1, 4), (2, 32))),
        "saved_short": centred(seeds[1], (LAYERS, MICRO, SEQ, D), 0.6, 3.5, ((0, 2), (2, 4), (3, 32))),
        "saved_medium": centred(seeds[2], (LAYERS, MICRO, SEQ, D), 0.6, 3.5, ((0, 2), (2, 4), (3, 32))),
        "out_weight": centred(seeds[3], (LAYERS, D, D), D ** -0.5, 0.0625, ((0, 2), (1, 32))),
        "short_filter": centred(seeds[4], (LAYERS, SHORT_TAPS, D), 0.4, 2.5, ((0, 2), (2, 32)), jnp.float32),
        "medium_filter": centred(seeds[5], (LAYERS, MED_TAPS, D), 0.09, 0.5, ((0, 2), (2, 32)), jnp.float32),
        "proj_in": centred(seeds[6], (LAYERS, D, RANK), D ** -0.5, 0.0625, ((0, 2), (1, 32))),
        "proj_out": centred(seeds[7], (LAYERS, D, RANK), D ** -0.5, 0.0625, ((0, 2),)),
    }


def adjoint_filter(values, filter_taps):
    tap_count = filter_taps.shape[0]
    length = values.shape[1]
    padded = jnp.pad(values, ((0, 0), (0, tap_count - 1), (0, 0)))

    def add_tap(tap_index, total):
        offset = jnp.asarray(tap_index).astype(jnp.int32)
        window = lax.dynamic_slice_in_dim(padded, offset, length, 1)
        coefficient = lax.dynamic_index_in_dim(filter_taps, offset, 0, keepdims=False)
        return total + coefficient * window
    return lax.fori_loop(0, tap_count, add_tap, jnp.zeros_like(values))

def reference(cotangent, saved_short, saved_medium, out_weight, short_filter, medium_filter, proj_in, proj_out):
    gradient = cotangent
    norm_factor = 1.0 / math.sqrt(SEQ)
    results = []
    for layer_index in range(LAYERS - 1, -1, -1):
        short_act = saved_short[layer_index].astype(jnp.float32)
        medium_act = saved_medium[layer_index].astype(jnp.float32)
        gated = (short_act * medium_act).astype(jnp.bfloat16)
        flat_grad = gradient.reshape(MICRO * SEQ, D)
        back_low = jnp.dot(flat_grad, out_weight[layer_index].T, preferred_element_type=jnp.float32).astype(jnp.bfloat16)
        back_low = lax.optimization_barrier(back_low)
        back_grad = back_low.astype(jnp.float32).reshape(MICRO, SEQ, D)
        gate_short = back_grad * medium_act
        gate_medium = back_grad * short_act
        in_side = jnp.dot(gated.reshape(MICRO * SEQ, D), proj_in[layer_index], preferred_element_type=jnp.float32).reshape(MICRO, SEQ, RANK)
        out_side = jnp.dot(flat_grad, proj_out[layer_index], preferred_element_type=jnp.float32).reshape(MICRO, SEQ, RANK)
        results.append(jnp.einsum('mtr,mtq->mrq', in_side, out_side, precision=lax.Precision.HIGHEST) * norm_factor)
        adj_short = adjoint_filter(gate_short, short_filter[layer_index])
        adj_medium = adjoint_filter(gate_medium, medium_filter[layer_index])
        gradient = (gradient.astype(jnp.float32) + adj_short + adj_medium).astype(jnp.bfloat16)
    return jnp.stack(results[::-1])
```

```python
import math

import jax
import jax.numpy as jnp
from jax import lax
from jax.sharding import PartitionSpec as P

X_CHIPS = 4


def xor_pairs(size, by):
    return [(i, i ^ by) for i in range(size)]


def swapped(array):
    return lax.ppermute(array, "pipe", [(0, 1), (1, 0)])


def from_section(array, source):
    got = lax.ppermute(array, "pipe", [(source, 1 - source)])
    return jnp.where(lax.axis_index("pipe") == source, array, got)


def quad_sum(value, axis, strides):
    size = lax.axis_size(axis)
    one, two, three = (lax.ppermute(value, axis, xor_pairs(size, by)) for by in strides)
    return (value + one) + (two + three)


def sum_everywhere(value):
    size = lax.axis_size("tensor")
    value = quad_sum(value, "tensor", (1, 2, 3))
    value = quad_sum(value, "tensor", (4, 8, 12))
    value = value + lax.ppermute(value, "tensor", xor_pairs(size, 16))
    return quad_sum(value, "dp", (1, 2, 3))


def tensor_sum(part):
    size = lax.axis_size("tensor")
    rows, width = part.shape
    pieces = lax.all_to_all(
        part.reshape(size, rows // size, width), "tensor", 0, 0, tiled=True
    )
    own = jnp.sum(pieces, axis=0)
    spread = jnp.broadcast_to(own[None], (size,) + own.shape)
    return lax.all_to_all(spread, "tensor", 0, 0, tiled=True).reshape(rows, width)


def adjoint_filter(extended, filter_taps):
    return lax.conv_general_dilated(
        extended,
        filter_taps[:, None, :],
        (1,),
        "VALID",
        dimension_numbers=("NWC", "WIO", "NWC"),
        feature_group_count=extended.shape[2],
        precision=lax.Precision.HIGHEST,
    )


def previous_rim(array):
    size = lax.axis_size("dp")
    return lax.ppermute(array, "dp", [(i, i - 1) for i in range(1, size)])


def body(
    cotangent, saved_short, saved_medium, out_weight, short_filter, medium_filter, proj_in, proj_out
):
    core = lax.axis_index("pipe")
    shard = lax.axis_index("tensor")
    micro_count, seq_dev, width = cotangent.shape
    rank = proj_in.shape[2]
    norm_factor = 1.0 / math.sqrt(seq_dev * lax.axis_size("dp"))
    own_grad = jnp.where(core == 1, cotangent[1], cotangent[0])
    gathered = lax.all_gather(own_grad, "tensor", axis=1, tiled=True)

    weight = from_section(out_weight[0], 1)
    saved = jnp.stack([saved_short[0, 0], saved_medium[0, 0]])
    saved_got = lax.ppermute(saved, "pipe", [(1, 0)])
    short_act = jnp.where(core == 1, saved_short[0, 1], saved_got[0]).astype(jnp.float32)
    medium_act = jnp.where(core == 1, saved_medium[0, 1], saved_got[1]).astype(jnp.float32)
    taps = from_section(jnp.concatenate([short_filter[0], medium_filter[0]], axis=0), 1)
    short_count = short_filter.shape[1]
    short_taps, medium_taps = taps[:short_count], taps[short_count:]

    gated = (saved_short[0].astype(jnp.float32) * saved_medium[0].astype(jnp.float32)).astype(
        jnp.bfloat16
    )
    in_part = jnp.dot(
        gated.reshape(micro_count * seq_dev, width), proj_in[0], preferred_element_type=jnp.float32
    )
    in_full = tensor_sum(in_part).reshape(micro_count, seq_dev, rank)
    in_kept = jnp.where(core == 1, in_full[1], in_full[0])
    in_got = swapped(jnp.where(core == 1, in_full[0], in_full[1]))
    in_low = jnp.where(core == 1, in_got, in_kept)
    in_high = jnp.where(core == 1, in_kept, in_got)

    basis = lax.dynamic_slice_in_dim(proj_out[0], shard * width, width, axis=0)
    basis_got = swapped(basis)
    basis_low = jnp.where(core == 1, basis_got, basis)
    basis_high = jnp.where(core == 1, basis, basis_got)

    def outer(in_side, out_part):
        return lax.dot_general(
            in_side, out_part, (((0,), (0,)), ((), ())), precision=lax.Precision.HIGHEST
        )

    part_high = outer(in_high, jnp.dot(own_grad, basis_high, preferred_element_type=jnp.float32))

    back_low = lax.dot_general(
        gathered, weight, (((1,), (1,)), ((), ())), preferred_element_type=jnp.float32
    ).astype(jnp.bfloat16)
    back_grad = lax.optimization_barrier(back_low).astype(jnp.float32)
    gate_short = back_grad * medium_act
    gate_medium = back_grad * short_act
    short_rim, medium_rim = short_count - 1, medium_filter.shape[1] - 1
    rims = previous_rim(
        jnp.concatenate([gate_short[:short_rim], gate_medium[:medium_rim]], axis=0).astype(
            jnp.bfloat16
        )
    ).astype(jnp.float32)
    adj_short = adjoint_filter(
        jnp.concatenate([gate_short, rims[:short_rim]], axis=0)[None], short_taps
    )[0]
    adj_medium = adjoint_filter(
        jnp.concatenate([gate_medium, rims[short_rim:]], axis=0)[None], medium_taps
    )[0]
    low_grad = (own_grad.astype(jnp.float32) + adj_short + adj_medium).astype(jnp.bfloat16)
    part_low = outer(in_low, jnp.dot(low_grad, basis_low, preferred_element_type=jnp.float32))

    sums = sum_everywhere(jnp.stack([part_low, part_high])) * norm_factor
    kept = jnp.where(core == 1, sums[1], sums[0])
    got = swapped(jnp.where(core == 1, sums[0], sums[1]))
    return jnp.where(core == 1, jnp.stack([got, kept]), jnp.stack([kept, got]))[None]


def solution(mesh):
    in_specs = (
        P(None, "dp", "tensor"),
        P("pipe", None, "dp", "tensor"),
        P("pipe", None, "dp", "tensor"),
        P("pipe", "tensor", None),
        P("pipe", None, "tensor"),
        P("pipe", None, "tensor"),
        P("pipe", "tensor", None),
        P("pipe", None, None),
    )
    out_specs = P("pipe", None, None, None)
    return jax.shard_map(body, mesh=mesh, in_specs=in_specs, out_specs=out_specs, check_vma=False)
```

```python
import math

import jax
import jax.numpy as jnp
from jax import lax
from jax.sharding import PartitionSpec as P

X_CHIPS = 4
Z_ORDER = (0, 1, -1, 2, -2, 3, -3, 4)


def xor_pairs(size, by):
    return [(i, i ^ by) for i in range(size)]


def swapped(array):
    return lax.ppermute(array, "pipe", [(0, 1), (1, 0)])


def from_section(array, source):
    got = lax.ppermute(array, "pipe", [(source, 1 - source)])
    return jnp.where(lax.axis_index("pipe") == source, array, got)


def quad_sum(value, axis, strides):
    size = lax.axis_size(axis)
    one, two, three = (lax.ppermute(value, axis, xor_pairs(size, by)) for by in strides)
    return (value + one) + (two + three)


def sum_everywhere(value):
    size = lax.axis_size("tensor")
    value = quad_sum(value, "tensor", (1, 2, 3))
    value = quad_sum(value, "tensor", (4, 8, 12))
    value = value + lax.ppermute(value, "tensor", xor_pairs(size, 16))
    return quad_sum(value, "dp", (1, 2, 3))


def tensor_sum(part):
    size = lax.axis_size("tensor")
    rows, width = part.shape
    place = lax.axis_index("tensor") % X_CHIPS
    quarters = part.reshape(X_CHIPS, rows // X_CHIPS, width)

    def quarter(index):
        return lax.dynamic_index_in_dim(quarters, index, 0, keepdims=False)

    got = [
        lax.ppermute(quarter(place ^ by), "tensor", xor_pairs(size, by)) for by in (1, 2, 3)
    ]
    own = (quarter(place) + got[0]) + (got[1] + got[2])
    own = quad_sum(own, "tensor", (4, 8, 12))
    own = own + lax.ppermute(own, "tensor", xor_pairs(size, 16))
    others = jnp.stack(
        [own] + [lax.ppermute(own, "tensor", xor_pairs(size, by)) for by in (1, 2, 3)]
    )
    ordered = [lax.dynamic_index_in_dim(others, place ^ q, 0, keepdims=False) for q in range(4)]
    return jnp.concatenate(ordered, axis=0)


def along_z(array, by):
    size = lax.axis_size("tensor")
    return lax.ppermute(array, "tensor", [(i, (i + X_CHIPS * by) % size) for i in range(size)])


def z_ring(block):
    half = block.shape[0] // 2
    blocks = {0: block}
    for step in (1, 2, 3):
        blocks[step] = along_z(blocks[step - 1], 1)
        blocks[-step] = along_z(blocks[1 - step], -1)
    blocks[4] = jnp.concatenate(
        [along_z(blocks[3][:half], 1), along_z(blocks[-3][half:], -1)], axis=0
    )
    return blocks


def weight_pieces(weight, place):
    size = lax.axis_size("tensor")
    width = weight.shape[0]
    x_place, z_place = place % X_CHIPS, place // X_CHIPS
    z_size = size // X_CHIPS
    pieces = []
    for by in range(X_CHIPS):
        columns = [
            lax.dynamic_slice_in_dim(
                weight, (((z_place - d) % z_size) * X_CHIPS + (x_place ^ by)) * width, width, axis=1
            )
            for d in Z_ORDER
        ]
        piece = jnp.concatenate(columns, axis=1)
        if by:
            pairs = [(size + i, size + (i ^ by)) for i in range(size)]
            piece = lax.ppermute(piece, ("pipe", "tensor"), pairs)
        pieces.append(from_section(piece, 1))
    return pieces


def back_product(block, weight, place):
    size = lax.axis_size("tensor")
    pieces = weight_pieces(weight, place)
    blocks = z_ring(block)
    width = block.shape[1]
    split = 5
    near = jnp.concatenate([blocks[d] for d in Z_ORDER[:split]], axis=1)
    far = jnp.concatenate([blocks[d] for d in Z_ORDER[split:]], axis=1)

    def product(rows, columns):
        return lax.dot_general(
            rows, columns, (((1,), (1,)), ((), ())), preferred_element_type=jnp.float32
        )

    parts = [
        product(near, piece[:, : split * width]) + product(far, piece[:, split * width :])
        for piece in pieces
    ]
    got = [
        lax.ppermute(part.astype(jnp.bfloat16), "tensor", xor_pairs(size, by)).astype(jnp.float32)
        for by, part in enumerate(parts)
        if by
    ]
    return parts[0] + (got[0] + got[1] + got[2])


def adjoint_filter(extended, filter_taps):
    return lax.conv_general_dilated(
        extended,
        filter_taps[:, None, :],
        (1,),
        "VALID",
        dimension_numbers=("NWC", "WIO", "NWC"),
        feature_group_count=extended.shape[2],
        precision=lax.Precision.HIGHEST,
    )


def previous_rim(array):
    size = lax.axis_size("dp")
    return lax.ppermute(array, "dp", [(i, i - 1) for i in range(1, size)])


def body(
    cotangent, saved_short, saved_medium, out_weight, short_filter, medium_filter, proj_in, proj_out
):
    core = lax.axis_index("pipe")
    shard = lax.axis_index("tensor")
    micro_count, seq_dev, width = cotangent.shape
    rank = proj_in.shape[2]
    norm_factor = 1.0 / math.sqrt(seq_dev * lax.axis_size("dp"))
    own_grad = jnp.where(core == 1, cotangent[1], cotangent[0])
    saved = jnp.stack([saved_short[0, 0], saved_medium[0, 0]])
    saved_got = lax.ppermute(saved, "pipe", [(1, 0)])
    short_act = jnp.where(core == 1, saved_short[0, 1], saved_got[0]).astype(jnp.float32)
    medium_act = jnp.where(core == 1, saved_medium[0, 1], saved_got[1]).astype(jnp.float32)
    taps = from_section(jnp.concatenate([short_filter[0], medium_filter[0]], axis=0), 1)
    short_count = short_filter.shape[1]
    short_taps, medium_taps = taps[:short_count], taps[short_count:]

    gated = (saved_short[0].astype(jnp.float32) * saved_medium[0].astype(jnp.float32)).astype(
        jnp.bfloat16
    )
    in_part = jnp.dot(
        gated.reshape(micro_count * seq_dev, width), proj_in[0], preferred_element_type=jnp.float32
    )
    in_full = tensor_sum(in_part).reshape(micro_count, seq_dev, rank)
    in_kept = jnp.where(core == 1, in_full[1], in_full[0])
    in_got = swapped(jnp.where(core == 1, in_full[0], in_full[1]))
    in_low = jnp.where(core == 1, in_got, in_kept)
    in_high = jnp.where(core == 1, in_kept, in_got)

    basis = lax.dynamic_slice_in_dim(proj_out[0], shard * width, width, axis=0)
    basis_got = swapped(basis)
    basis_low = jnp.where(core == 1, basis_got, basis)
    basis_high = jnp.where(core == 1, basis, basis_got)

    def outer(in_side, out_part):
        return lax.dot_general(
            in_side, out_part, (((0,), (0,)), ((), ())), precision=lax.Precision.HIGHEST
        )

    part_high = outer(in_high, jnp.dot(own_grad, basis_high, preferred_element_type=jnp.float32))

    back_low = back_product(own_grad, out_weight[0], shard).astype(jnp.bfloat16)
    back_grad = lax.optimization_barrier(back_low).astype(jnp.float32)
    gate_short = back_grad * medium_act
    gate_medium = back_grad * short_act
    short_rim, medium_rim = short_count - 1, medium_filter.shape[1] - 1
    rims = previous_rim(
        jnp.concatenate([gate_short[:short_rim], gate_medium[:medium_rim]], axis=0).astype(
            jnp.bfloat16
        )
    ).astype(jnp.float32)
    adj_short = adjoint_filter(
        jnp.concatenate([gate_short, rims[:short_rim]], axis=0)[None], short_taps
    )[0]
    adj_medium = adjoint_filter(
        jnp.concatenate([gate_medium, rims[short_rim:]], axis=0)[None], medium_taps
    )[0]
    low_grad = (own_grad.astype(jnp.float32) + adj_short + adj_medium).astype(jnp.bfloat16)
    part_low = outer(in_low, jnp.dot(low_grad, basis_low, preferred_element_type=jnp.float32))

    sums = sum_everywhere(jnp.stack([part_low, part_high])) * norm_factor
    kept = jnp.where(core == 1, sums[1], sums[0])
    got = swapped(jnp.where(core == 1, sums[0], sums[1]))
    return jnp.where(core == 1, jnp.stack([got, kept]), jnp.stack([kept, got]))[None]


def solution(mesh):
    in_specs = (
        P(None, "dp", "tensor"),
        P("pipe", None, "dp", "tensor"),
        P("pipe", None, "dp", "tensor"),
        P("pipe", "tensor", None),
        P("pipe", None, "tensor"),
        P("pipe", None, "tensor"),
        P("pipe", "tensor", None),
        P("pipe", None, None),
    )
    out_specs = P("pipe", None, None, None)
    return jax.shard_map(body, mesh=mesh, in_specs=in_specs, out_specs=out_specs, check_vma=False)
```

```python
import math

import jax
import jax.numpy as jnp
from jax import lax
from jax.experimental import pallas as pl
from jax.experimental.pallas import tpu as pltpu
from jax.sharding import PartitionSpec as P

X_CHIPS = 4
VMEM_BYTES = 40 * 1024 * 1024
TURNS = 8
CHUNK = 16


def xor_pairs(size, by):
    return [(i, i ^ by) for i in range(size)]


def swapped(array):
    return lax.ppermute(array, "pipe", [(0, 1), (1, 0)])


def from_section(array, source):
    got = lax.ppermute(array, "pipe", [(source, 1 - source)])
    return jnp.where(lax.axis_index("pipe") == source, array, got)


def quad_sum(value, axis, strides):
    size = lax.axis_size(axis)
    one, two, three = (lax.ppermute(value, axis, xor_pairs(size, by)) for by in strides)
    return (value + one) + (two + three)


def sum_everywhere(value):
    size = lax.axis_size("tensor")
    value = quad_sum(value, "tensor", (1, 2, 3))
    value = quad_sum(value, "tensor", (4, 8, 12))
    value = value + lax.ppermute(value, "tensor", xor_pairs(size, 16))
    return quad_sum(value, "dp", (1, 2, 3))


def tensor_sum(part):
    size = lax.axis_size("tensor")
    rows, width = part.shape
    place = lax.axis_index("tensor") % X_CHIPS
    quarters = part.reshape(X_CHIPS, rows // X_CHIPS, width)

    def quarter(index):
        return lax.dynamic_index_in_dim(quarters, index, 0, keepdims=False)

    got = [
        lax.ppermute(quarter(place ^ by), "tensor", xor_pairs(size, by)) for by in (1, 2, 3)
    ]
    own = (quarter(place) + got[0]) + (got[1] + got[2])
    own = quad_sum(own, "tensor", (4, 8, 12))
    own = own + lax.ppermute(own, "tensor", xor_pairs(size, 16))
    others = jnp.stack(
        [own] + [lax.ppermute(own, "tensor", xor_pairs(size, by)) for by in (1, 2, 3)]
    )
    ordered = [lax.dynamic_index_in_dim(others, place ^ q, 0, keepdims=False) for q in range(4)]
    return jnp.concatenate(ordered, axis=0)


def cut_weight(weight, place):
    rows, columns = weight.shape
    z_size = columns // rows // X_CHIPS

    block = rows // 4

    def kernel(place_ref, weight_ref, *pieces):
        for by in range(X_CHIPS):
            for z in range(z_size):
                start = pl.multiple_of((z * X_CHIPS + (place_ref[0] ^ by)) * rows, rows)
                pieces[by][:, z * rows : (z + 1) * rows] = weight_ref[:, pl.ds(start, rows)]

    return pl.pallas_call(
        kernel,
        grid=(rows // block,),
        out_shape=[jax.ShapeDtypeStruct((rows, columns // X_CHIPS), weight.dtype)] * X_CHIPS,
        in_specs=[
            pl.BlockSpec(memory_space=pltpu.SMEM),
            pl.BlockSpec((block, columns), lambda step: (step, 0)),
        ],
        out_specs=[pl.BlockSpec((block, columns // X_CHIPS), lambda step: (step, 0))] * X_CHIPS,
        compiler_params=pltpu.CompilerParams(vmem_limit_bytes=VMEM_BYTES),
        name="cut_weight",
    )(place.reshape(1), weight)


def weight_pieces(weight, place):
    size = lax.axis_size("tensor")
    pieces = list(cut_weight(weight, place % X_CHIPS))
    for by in (2, 1, 3):
        pairs = [(size + i, size + (i ^ by)) for i in range(size)]
        pieces[by] = lax.ppermute(pieces[by], ("pipe", "tensor"), pairs)
    return lax.optimization_barrier([from_section(piece, 1) for piece in pieces])


def back_parts(block, weight, place):
    size = lax.axis_size("tensor")
    columns = [[z * X_CHIPS + x for z in range(size // X_CHIPS)] for x in range(X_CHIPS)]
    gathered = lax.all_gather(block, "tensor", axis=1, tiled=True, axis_index_groups=columns)
    parts = [
        lax.dot_general(
            gathered, piece, (((1,), (1,)), ((), ())), preferred_element_type=jnp.float32
        )
        for piece in weight_pieces(weight, place)
    ]
    return parts[:1] + [
        lax.ppermute(parts[by].astype(jnp.bfloat16), "tensor", xor_pairs(size, by))
        for by in (1, 2, 3)
    ]


def shifted_rows(extended, tap_count):
    total, width = extended.shape
    length = total - tap_count

    def kernel(in_ref, out_ref, turned_ref):
        turned_ref[...] = in_ref[...].T

        def step(group, carry):
            turned = turned_ref[...]
            for tap in range(TURNS):
                start = pl.multiple_of((group * TURNS + tap) * width, width)
                rows = pltpu.roll(turned, tap, 1) if tap else turned
                out_ref[pl.ds(start, width), :] = rows[:, tap_count:].astype(jnp.bfloat16)
            turned_ref[...] = pltpu.roll(turned, TURNS, 1)
            return carry

        lax.fori_loop(0, tap_count // TURNS, step, 0)

    return pl.pallas_call(
        kernel,
        out_shape=jax.ShapeDtypeStruct((tap_count * width, length), jnp.bfloat16),
        scratch_shapes=[pltpu.VMEM((width, total), jnp.float32)],
        compiler_params=pltpu.CompilerParams(vmem_limit_bytes=VMEM_BYTES),
        name="shifted_rows",
    )(extended)


def filtered_outer(parts, short_act, medium_act, shifted, short_taps, medium_taps, direct, basis):
    length, width = short_act.shape
    rank = direct.shape[0]
    short_count, tap_count = short_taps.shape[0], medium_taps.shape[0]
    steps = tap_count // CHUNK

    def kernel(
        part_ref, one_ref, two_ref, three_ref, short_ref, medium_ref, shifted_ref, short_taps_ref,
        medium_taps_ref, direct_ref, basis_ref, out_ref, gate_ref, sum_ref,
    ):
        step = pl.program_id(0)

        @pl.when(step == 0)
        def _():
            total = part_ref[...] + (
                one_ref[...].astype(jnp.float32)
                + two_ref[...].astype(jnp.float32)
                + three_ref[...].astype(jnp.float32)
            )
            back = total.astype(jnp.bfloat16).astype(jnp.float32)
            gate_ref[...] = (back * short_ref[...].astype(jnp.float32)).astype(jnp.bfloat16)
            gate_short = (back * medium_ref[...].astype(jnp.float32)).astype(jnp.bfloat16)
            product = jnp.dot(
                shifted_ref[: short_count * rank, :], gate_short, preferred_element_type=jnp.float32
            )
            total = direct_ref[...]
            for tap in range(short_count):
                total += short_taps_ref[tap : tap + 1, :] * product[tap * rank : (tap + 1) * rank]
            sum_ref[...] = total

        product = jnp.dot(shifted_ref[...], gate_ref[...], preferred_element_type=jnp.float32)
        total = sum_ref[...]
        taps = medium_taps_ref[...]
        for tap in range(CHUNK):
            total += taps[tap : tap + 1, :] * product[tap * rank : (tap + 1) * rank]
        sum_ref[...] = total

        @pl.when(step == steps - 1)
        def _():
            out_ref[...] = jnp.dot(
                sum_ref[...], basis_ref[...].astype(jnp.float32), precision=lax.Precision.HIGHEST
            )

    def whole(array):
        return pl.BlockSpec(array.shape, lambda step: (0, 0))

    parts = list(parts) + [short_act, medium_act]
    return pl.pallas_call(
        kernel,
        grid=(steps,),
        out_shape=jax.ShapeDtypeStruct((rank, basis.shape[1]), jnp.float32),
        in_specs=[whole(part) for part in parts]
        + [
            pl.BlockSpec((CHUNK * rank, length), lambda step: (step, 0)),
            whole(short_taps),
            pl.BlockSpec((CHUNK, width), lambda step: (step, 0)),
            whole(direct),
            whole(basis),
        ],
        out_specs=pl.BlockSpec((rank, basis.shape[1]), lambda step: (0, 0)),
        scratch_shapes=[
            pltpu.VMEM((length, width), jnp.bfloat16),
            pltpu.VMEM((rank, width), jnp.float32),
        ],
        compiler_params=pltpu.CompilerParams(vmem_limit_bytes=VMEM_BYTES),
        name="filtered_outer",
    )(*parts, shifted, short_taps, medium_taps, direct, basis)


def with_rim_before(array, count):
    size = lax.axis_size("dp")
    rim = lax.ppermute(array[-count:], "dp", [(i, i + 1) for i in range(size - 1)])
    return jnp.concatenate([rim, array], axis=0)


def body(
    cotangent, saved_short, saved_medium, out_weight, short_filter, medium_filter, proj_in, proj_out
):
    core = lax.axis_index("pipe")
    shard = lax.axis_index("tensor")
    micro_count, seq_dev, width = cotangent.shape
    rank = proj_in.shape[2]
    norm_factor = 1.0 / math.sqrt(seq_dev * lax.axis_size("dp"))
    own_grad = jnp.where(core == 1, cotangent[1], cotangent[0])
    saved = jnp.stack([saved_short[0, 0], saved_medium[0, 0]])
    saved_got = lax.ppermute(saved, "pipe", [(1, 0)])
    short_act = jnp.where(core == 1, saved_short[0, 1], saved_got[0])
    medium_act = jnp.where(core == 1, saved_medium[0, 1], saved_got[1])
    taps = from_section(jnp.concatenate([short_filter[0], medium_filter[0]], axis=0), 1)
    short_count = short_filter.shape[1]
    short_taps, medium_taps = taps[:short_count], taps[short_count:]

    gated = (saved_short[0].astype(jnp.float32) * saved_medium[0].astype(jnp.float32)).astype(
        jnp.bfloat16
    )
    in_part = jnp.dot(
        gated.reshape(micro_count * seq_dev, width), proj_in[0], preferred_element_type=jnp.float32
    )
    in_full = tensor_sum(in_part).reshape(micro_count, seq_dev, rank)
    in_kept = jnp.where(core == 1, in_full[1], in_full[0])
    in_got = swapped(jnp.where(core == 1, in_full[0], in_full[1]))
    in_low = jnp.where(core == 1, in_got, in_kept)
    in_high = jnp.where(core == 1, in_kept, in_got)

    basis = lax.dynamic_slice_in_dim(proj_out[0], shard * width, width, axis=0)
    basis_got = swapped(basis)
    basis_low = jnp.where(core == 1, basis_got, basis)
    basis_high = jnp.where(core == 1, basis, basis_got)

    def outer(in_side, out_part):
        return lax.dot_general(
            in_side, out_part, (((0,), (0,)), ((), ())), precision=lax.Precision.HIGHEST
        )

    part_high = outer(in_high, jnp.dot(own_grad, basis_high, preferred_element_type=jnp.float32))

    shifted = shifted_rows(
        with_rim_before(in_low, medium_taps.shape[0]), medium_taps.shape[0]
    )
    direct = outer(in_low, own_grad.astype(jnp.float32))
    part_low = filtered_outer(
        back_parts(own_grad, out_weight[0], shard),
        short_act, medium_act, shifted, short_taps, medium_taps, direct, basis_low,
    )

    sums = sum_everywhere(jnp.stack([part_low, part_high])) * norm_factor
    kept = jnp.where(core == 1, sums[1], sums[0])
    got = swapped(jnp.where(core == 1, sums[0], sums[1]))
    return jnp.where(core == 1, jnp.stack([got, kept]), jnp.stack([kept, got]))[None]


def solution(mesh):
    in_specs = (
        P(None, "dp", "tensor"),
        P("pipe", None, "dp", "tensor"),
        P("pipe", None, "dp", "tensor"),
        P("pipe", "tensor", None),
        P("pipe", None, "tensor"),
        P("pipe", None, "tensor"),
        P("pipe", "tensor", None),
        P("pipe", None, None),
    )
    out_specs = P("pipe", None, None, None)
    return jax.shard_map(body, mesh=mesh, in_specs=in_specs, out_specs=out_specs, check_vma=False)
```

```python
import math

import jax
import jax.numpy as jnp
from jax import lax
from jax.experimental import pallas as pl
from jax.experimental.pallas import tpu as pltpu
from jax.sharding import PartitionSpec as P

X_CHIPS = 4
VMEM_BYTES = 40 * 1024 * 1024
TURNS = 16
CHUNK = 16


def xor_pairs(size, by):
    return [(i, i ^ by) for i in range(size)]


def swapped(array):
    return lax.ppermute(array, "pipe", [(0, 1), (1, 0)])


def from_section(array, source):
    got = lax.ppermute(array, "pipe", [(source, 1 - source)])
    return jnp.where(lax.axis_index("pipe") == source, array, got)


def quad_sum(value, axis, strides):
    size = lax.axis_size(axis)
    one, two, three = (lax.ppermute(value, axis, xor_pairs(size, by)) for by in strides)
    return (value + one) + (two + three)


def sum_everywhere(value):
    size = lax.axis_size("tensor")
    value = quad_sum(value, "tensor", (1, 2, 3))
    value = quad_sum(value, "tensor", (4, 8, 12))
    value = value + lax.ppermute(value, "tensor", xor_pairs(size, 16))
    return quad_sum(value, "dp", (1, 2, 3))


def tensor_sum(part):
    size = lax.axis_size("tensor")
    rows, width = part.shape
    place = lax.axis_index("tensor") % X_CHIPS
    quarters = part.reshape(X_CHIPS, rows // X_CHIPS, width)

    def quarter(index):
        return lax.dynamic_index_in_dim(quarters, index, 0, keepdims=False)

    got = [
        lax.ppermute(quarter(place ^ by), "tensor", xor_pairs(size, by)) for by in (1, 2, 3)
    ]
    own = (quarter(place) + got[0]) + (got[1] + got[2])
    own = quad_sum(own, "tensor", (4, 8, 12))
    own = own + lax.ppermute(own, "tensor", xor_pairs(size, 16))
    others = jnp.stack(
        [own] + [lax.ppermute(own, "tensor", xor_pairs(size, by)) for by in (1, 2, 3)]
    )
    ordered = [lax.dynamic_index_in_dim(others, place ^ q, 0, keepdims=False) for q in range(4)]
    return jnp.concatenate(ordered, axis=0)


def cut_weight(weight, place):
    rows, columns = weight.shape
    z_size = columns // rows // X_CHIPS

    block = rows // 4

    def kernel(place_ref, weight_ref, *pieces):
        for by in range(X_CHIPS):
            for z in range(z_size):
                start = pl.multiple_of((z * X_CHIPS + (place_ref[0] ^ by)) * rows, rows)
                pieces[by][:, z * rows : (z + 1) * rows] = weight_ref[:, pl.ds(start, rows)]

    return pl.pallas_call(
        kernel,
        grid=(rows // block,),
        out_shape=[jax.ShapeDtypeStruct((rows, columns // X_CHIPS), weight.dtype)] * X_CHIPS,
        in_specs=[
            pl.BlockSpec(memory_space=pltpu.SMEM),
            pl.BlockSpec((block, columns), lambda step: (step, 0)),
        ],
        out_specs=[pl.BlockSpec((block, columns // X_CHIPS), lambda step: (step, 0))] * X_CHIPS,
        compiler_params=pltpu.CompilerParams(vmem_limit_bytes=VMEM_BYTES),
        name="cut_weight",
    )(place.reshape(1), weight)


def weight_pieces(weight, place):
    size = lax.axis_size("tensor")
    pieces = list(cut_weight(weight, place % X_CHIPS))
    for by in (2, 1, 3):
        pairs = [(size + i, size + (i ^ by)) for i in range(size)]
        pieces[by] = lax.ppermute(pieces[by], ("pipe", "tensor"), pairs)
    return lax.optimization_barrier([from_section(piece, 1) for piece in pieces])


def back_parts(block, weight, place):
    size = lax.axis_size("tensor")
    columns = [[z * X_CHIPS + x for z in range(size // X_CHIPS)] for x in range(X_CHIPS)]
    gathered = lax.all_gather(block, "tensor", axis=1, tiled=True, axis_index_groups=columns)
    parts = [
        lax.dot_general(
            gathered, piece, (((1,), (1,)), ((), ())), preferred_element_type=jnp.float32
        )
        for piece in weight_pieces(weight, place)
    ]
    return parts[:1] + [
        lax.ppermute(parts[by].astype(jnp.bfloat16), "tensor", xor_pairs(size, by))
        for by in (1, 2, 3)
    ]


def shifted_rows(extended, tap_count):
    total, width = extended.shape
    length = total - tap_count

    def kernel(in_ref, out_ref, turned_ref):
        @pl.when(pl.program_id(0) == 0)
        def _():
            turned_ref[...] = in_ref[...].T

        turned = turned_ref[...]
        for tap in range(TURNS):
            rows = pltpu.roll(turned, tap, 1) if tap else turned
            out_ref[tap * width : (tap + 1) * width, :] = rows[:, tap_count:].astype(jnp.bfloat16)
        turned_ref[...] = pltpu.roll(turned, TURNS, 1)

    return pl.pallas_call(
        kernel,
        grid=(tap_count // TURNS,),
        out_shape=pltpu.HBM((tap_count * width, length), jnp.bfloat16),
        in_specs=[pl.BlockSpec((total, width), lambda step: (0, 0))],
        out_specs=pl.BlockSpec((TURNS * width, length), lambda step: (step, 0)),
        scratch_shapes=[pltpu.VMEM((width, total), jnp.float32)],
        compiler_params=pltpu.CompilerParams(vmem_limit_bytes=VMEM_BYTES),
        name="shifted_rows",
    )(extended)


def filtered_outer(parts, short_act, medium_act, shifted, short_taps, medium_taps, direct, basis):
    length, width = short_act.shape
    rank = direct.shape[0]
    short_count, tap_count = short_taps.shape[0], medium_taps.shape[0]
    steps = tap_count // CHUNK

    def kernel(
        part_ref, one_ref, two_ref, three_ref, short_ref, medium_ref, shifted_ref, short_taps_ref,
        medium_taps_ref, direct_ref, basis_ref, out_ref, gate_ref, sum_ref,
    ):
        step = pl.program_id(0)

        @pl.when(step == 0)
        def _():
            total = part_ref[...] + (
                one_ref[...].astype(jnp.float32)
                + two_ref[...].astype(jnp.float32)
                + three_ref[...].astype(jnp.float32)
            )
            back = total.astype(jnp.bfloat16).astype(jnp.float32)
            gate_ref[...] = (back * short_ref[...].astype(jnp.float32)).astype(jnp.bfloat16)
            gate_short = (back * medium_ref[...].astype(jnp.float32)).astype(jnp.bfloat16)
            product = jnp.dot(
                shifted_ref[: short_count * rank, :], gate_short, preferred_element_type=jnp.float32
            )
            total = direct_ref[...]
            for tap in range(short_count):
                total += short_taps_ref[tap : tap + 1, :] * product[tap * rank : (tap + 1) * rank]
            sum_ref[...] = total

        product = jnp.dot(shifted_ref[...], gate_ref[...], preferred_element_type=jnp.float32)
        total = sum_ref[...]
        taps = medium_taps_ref[...]
        for tap in range(CHUNK):
            total += taps[tap : tap + 1, :] * product[tap * rank : (tap + 1) * rank]
        sum_ref[...] = total

        @pl.when(step == steps - 1)
        def _():
            out_ref[...] = jnp.dot(
                sum_ref[...], basis_ref[...].astype(jnp.float32), precision=lax.Precision.HIGHEST
            )

    def whole(array):
        return pl.BlockSpec(array.shape, lambda step: (0, 0))

    parts = list(parts) + [short_act, medium_act]
    return pl.pallas_call(
        kernel,
        grid=(steps,),
        out_shape=jax.ShapeDtypeStruct((rank, basis.shape[1]), jnp.float32),
        in_specs=[whole(part) for part in parts]
        + [
            pl.BlockSpec((CHUNK * rank, length), lambda step: (step, 0)),
            whole(short_taps),
            pl.BlockSpec((CHUNK, width), lambda step: (step, 0)),
            whole(direct),
            whole(basis),
        ],
        out_specs=pl.BlockSpec((rank, basis.shape[1]), lambda step: (0, 0)),
        scratch_shapes=[
            pltpu.VMEM((length, width), jnp.bfloat16),
            pltpu.VMEM((rank, width), jnp.float32),
        ],
        compiler_params=pltpu.CompilerParams(vmem_limit_bytes=VMEM_BYTES),
        name="filtered_outer",
    )(*parts, shifted, short_taps, medium_taps, direct, basis)


def with_rim_before(array, count):
    size = lax.axis_size("dp")
    rim = lax.ppermute(array[-count:], "dp", [(i, i + 1) for i in range(size - 1)])
    return jnp.concatenate([rim, array], axis=0)


def body(
    cotangent, saved_short, saved_medium, out_weight, short_filter, medium_filter, proj_in, proj_out
):
    core = lax.axis_index("pipe")
    shard = lax.axis_index("tensor")
    micro_count, seq_dev, width = cotangent.shape
    rank = proj_in.shape[2]
    norm_factor = 1.0 / math.sqrt(seq_dev * lax.axis_size("dp"))
    own_grad = jnp.where(core == 1, cotangent[1], cotangent[0])
    own_grad, saved_short, saved_medium = lax.optimization_barrier(
        (own_grad, saved_short, saved_medium)
    )
    saved = jnp.stack([saved_short[0, 0], saved_medium[0, 0]])
    saved_got = lax.ppermute(saved, "pipe", [(1, 0)])
    short_act = jnp.where(core == 1, saved_short[0, 1], saved_got[0])
    medium_act = jnp.where(core == 1, saved_medium[0, 1], saved_got[1])
    taps = from_section(jnp.concatenate([short_filter[0], medium_filter[0]], axis=0), 1)
    short_count = short_filter.shape[1]
    short_taps, medium_taps = taps[:short_count], taps[short_count:]

    gated = (saved_short[0].astype(jnp.float32) * saved_medium[0].astype(jnp.float32)).astype(
        jnp.bfloat16
    )
    in_part = jnp.dot(
        gated.reshape(micro_count * seq_dev, width), proj_in[0], preferred_element_type=jnp.float32
    )
    in_full = tensor_sum(in_part).reshape(micro_count, seq_dev, rank)
    in_kept = jnp.where(core == 1, in_full[1], in_full[0])
    in_got = swapped(jnp.where(core == 1, in_full[0], in_full[1]))
    in_low = jnp.where(core == 1, in_got, in_kept)
    in_high = jnp.where(core == 1, in_kept, in_got)

    basis = lax.dynamic_slice_in_dim(proj_out[0], shard * width, width, axis=0)
    basis_got = swapped(basis)
    basis_low = jnp.where(core == 1, basis_got, basis)
    basis_high = jnp.where(core == 1, basis, basis_got)

    def outer(in_side, out_part):
        return lax.dot_general(
            in_side, out_part, (((0,), (0,)), ((), ())), precision=lax.Precision.HIGHEST
        )

    part_high = outer(in_high, jnp.dot(own_grad, basis_high, preferred_element_type=jnp.float32))

    shifted = shifted_rows(
        with_rim_before(in_low, medium_taps.shape[0]), medium_taps.shape[0]
    )
    direct = outer(in_low, own_grad.astype(jnp.float32))
    part_low = filtered_outer(
        back_parts(own_grad, out_weight[0], shard),
        short_act, medium_act, shifted, short_taps, medium_taps, direct, basis_low,
    )

    sums = sum_everywhere(jnp.stack([part_low, part_high])) * norm_factor
    kept = jnp.where(core == 1, sums[1], sums[0])
    got = swapped(jnp.where(core == 1, sums[0], sums[1]))
    return jnp.where(core == 1, jnp.stack([got, kept]), jnp.stack([kept, got]))[None]


def solution(mesh):
    in_specs = (
        P(None, "dp", "tensor"),
        P("pipe", None, "dp", "tensor"),
        P("pipe", None, "dp", "tensor"),
        P("pipe", "tensor", None),
        P("pipe", None, "tensor"),
        P("pipe", None, "tensor"),
        P("pipe", "tensor", None),
        P("pipe", None, None),
    )
    out_specs = P("pipe", None, None, None)
    return jax.shard_map(body, mesh=mesh, in_specs=in_specs, out_specs=out_specs, check_vma=False)
```

```python
import math

import jax
import jax.numpy as jnp
from jax import lax
from jax.experimental import pallas as pl
from jax.experimental.pallas import tpu as pltpu
from jax.sharding import PartitionSpec as P

X_CHIPS = 4
VMEM_BYTES = 40 * 1024 * 1024
TURNS = 16
CHUNK = 16


def xor_pairs(size, by):
    return [(i, i ^ by) for i in range(size)]


def swapped(array):
    return lax.ppermute(array, "pipe", [(0, 1), (1, 0)])


def from_section(array, source):
    got = lax.ppermute(array, "pipe", [(source, 1 - source)])
    return jnp.where(lax.axis_index("pipe") == source, array, got)


def quad_sum(value, axis, strides):
    size = lax.axis_size(axis)
    one, two, three = (lax.ppermute(value, axis, xor_pairs(size, by)) for by in strides)
    return (value + one) + (two + three)


def sum_everywhere(value):
    size = lax.axis_size("tensor")
    value = quad_sum(value, "tensor", (1, 2, 3))
    value = quad_sum(value, "tensor", (4, 8, 12))
    value = value + lax.ppermute(value, "tensor", xor_pairs(size, 16))
    return quad_sum(value, "dp", (1, 2, 3))


def tensor_sum(part):
    size = lax.axis_size("tensor")
    rows, width = part.shape
    place = lax.axis_index("tensor") % X_CHIPS
    quarters = part.reshape(X_CHIPS, rows // X_CHIPS, width)

    def quarter(index):
        return lax.dynamic_index_in_dim(quarters, index, 0, keepdims=False)

    got = [
        lax.ppermute(quarter(place ^ by), "tensor", xor_pairs(size, by)) for by in (1, 2, 3)
    ]
    own = (quarter(place) + got[0]) + (got[1] + got[2])
    own = quad_sum(own, "tensor", (4, 8, 12))
    own = own + lax.ppermute(own, "tensor", xor_pairs(size, 16))
    others = jnp.stack(
        [own] + [lax.ppermute(own, "tensor", xor_pairs(size, by)) for by in (1, 2, 3)]
    )
    ordered = [lax.dynamic_index_in_dim(others, place ^ q, 0, keepdims=False) for q in range(4)]
    return jnp.concatenate(ordered, axis=0)


def cut_weight(weight, place):
    rows, columns = weight.shape
    z_size = columns // rows // X_CHIPS

    block = rows // 4

    def kernel(place_ref, weight_ref, *pieces):
        for by in range(X_CHIPS):
            for z in range(z_size):
                start = pl.multiple_of((z * X_CHIPS + (place_ref[0] ^ by)) * rows, rows)
                pieces[by][:, z * rows : (z + 1) * rows] = weight_ref[:, pl.ds(start, rows)]

    return pl.pallas_call(
        kernel,
        grid=(rows // block,),
        out_shape=[jax.ShapeDtypeStruct((rows, columns // X_CHIPS), weight.dtype)] * X_CHIPS,
        in_specs=[
            pl.BlockSpec(memory_space=pltpu.SMEM),
            pl.BlockSpec((block, columns), lambda step: (step, 0)),
        ],
        out_specs=[pl.BlockSpec((block, columns // X_CHIPS), lambda step: (step, 0))] * X_CHIPS,
        compiler_params=pltpu.CompilerParams(vmem_limit_bytes=VMEM_BYTES),
        name="cut_weight",
    )(place.reshape(1), weight)


def weight_pieces(weight, place):
    size = lax.axis_size("tensor")
    pieces = list(cut_weight(weight, place % X_CHIPS))
    for by in (2, 1, 3):
        pairs = [(size + i, size + (i ^ by)) for i in range(size)]
        pieces[by] = lax.ppermute(pieces[by], ("pipe", "tensor"), pairs)
    return lax.optimization_barrier([from_section(piece, 1) for piece in pieces])


def back_parts(block, weight, place):
    size = lax.axis_size("tensor")
    columns = [[z * X_CHIPS + x for z in range(size // X_CHIPS)] for x in range(X_CHIPS)]
    gathered = lax.all_gather(block, "tensor", axis=1, tiled=True, axis_index_groups=columns)
    parts = [
        lax.dot_general(
            gathered, piece, (((1,), (1,)), ((), ())), preferred_element_type=jnp.float32
        )
        for piece in weight_pieces(weight, place)
    ]
    return parts[:1] + [
        lax.ppermute(parts[by].astype(jnp.bfloat16), "tensor", xor_pairs(size, by))
        for by in (1, 2, 3)
    ]


def shifted_rows(extended, tap_count):
    total, width = extended.shape
    length = total - tap_count

    def kernel(in_ref, out_ref, turned_ref):
        @pl.when(pl.program_id(0) == 0)
        def _():
            turned_ref[...] = in_ref[...].T

        turned = turned_ref[...]
        for tap in range(TURNS):
            rows = pltpu.roll(turned, tap, 1) if tap else turned
            out_ref[tap * width : (tap + 1) * width, :] = rows[:, tap_count:].astype(jnp.bfloat16)
        turned_ref[...] = pltpu.roll(turned, TURNS, 1)

    return pl.pallas_call(
        kernel,
        grid=(tap_count // TURNS,),
        out_shape=pltpu.HBM((tap_count * width, length), jnp.bfloat16),
        in_specs=[pl.BlockSpec((total, width), lambda step: (0, 0))],
        out_specs=pl.BlockSpec((TURNS * width, length), lambda step: (step, 0)),
        scratch_shapes=[pltpu.VMEM((width, total), jnp.float32)],
        compiler_params=pltpu.CompilerParams(vmem_limit_bytes=VMEM_BYTES),
        name="shifted_rows",
    )(extended)


def filtered_outer(parts, short_act, medium_act, shifted, short_taps, medium_taps, direct, basis):
    length, width = short_act.shape
    rank = direct.shape[0]
    short_count, tap_count = short_taps.shape[0], medium_taps.shape[0]
    steps = tap_count // CHUNK

    def kernel(
        part_ref, one_ref, two_ref, three_ref, short_ref, medium_ref, shifted_ref, short_taps_ref,
        medium_taps_ref, direct_ref, basis_ref, out_ref, gate_ref, sum_ref,
    ):
        step = pl.program_id(0)

        @pl.when(step == 0)
        def _():
            total = part_ref[...] + (
                one_ref[...].astype(jnp.float32)
                + two_ref[...].astype(jnp.float32)
                + three_ref[...].astype(jnp.float32)
            )
            back = total.astype(jnp.bfloat16).astype(jnp.float32)
            gate_ref[...] = (back * short_ref[...].astype(jnp.float32)).astype(jnp.bfloat16)
            gate_short = (back * medium_ref[...].astype(jnp.float32)).astype(jnp.bfloat16)
            product = jnp.dot(
                shifted_ref[: short_count * rank, :], gate_short, preferred_element_type=jnp.float32
            )
            total = direct_ref[...]
            for tap in range(short_count):
                total += short_taps_ref[tap : tap + 1, :] * product[tap * rank : (tap + 1) * rank]
            sum_ref[...] = total

        product = jnp.dot(shifted_ref[...], gate_ref[...], preferred_element_type=jnp.float32)
        total = sum_ref[...]
        taps = medium_taps_ref[...]
        for tap in range(CHUNK):
            total += taps[tap : tap + 1, :] * product[tap * rank : (tap + 1) * rank]
        sum_ref[...] = total

        @pl.when(step == steps - 1)
        def _():
            out_ref[...] = jnp.dot(
                sum_ref[...], basis_ref[...].astype(jnp.float32), precision=lax.Precision.HIGHEST
            )

    def whole(array):
        return pl.BlockSpec(array.shape, lambda step: (0, 0))

    parts = list(parts) + [short_act, medium_act]
    return pl.pallas_call(
        kernel,
        grid=(steps,),
        out_shape=jax.ShapeDtypeStruct((rank, basis.shape[1]), jnp.float32),
        in_specs=[whole(part) for part in parts]
        + [
            pl.BlockSpec((CHUNK * rank, length), lambda step: (step, 0)),
            whole(short_taps),
            pl.BlockSpec((CHUNK, width), lambda step: (step, 0)),
            whole(direct),
            whole(basis),
        ],
        out_specs=pl.BlockSpec((rank, basis.shape[1]), lambda step: (0, 0)),
        scratch_shapes=[
            pltpu.VMEM((length, width), jnp.bfloat16),
            pltpu.VMEM((rank, width), jnp.float32),
        ],
        compiler_params=pltpu.CompilerParams(vmem_limit_bytes=VMEM_BYTES),
        name="filtered_outer",
    )(*parts, shifted, short_taps, medium_taps, direct, basis)


def with_rim_before(array, count):
    size = lax.axis_size("dp")
    rim = lax.ppermute(array[-count:], "dp", [(i, i + 1) for i in range(size - 1)])
    return jnp.concatenate([rim, array], axis=0)


def body(
    cotangent, saved_short, saved_medium, out_weight, short_filter, medium_filter, proj_in, proj_out
):
    core = lax.axis_index("pipe")
    shard = lax.axis_index("tensor")
    micro_count, seq_dev, width = cotangent.shape
    rank = proj_in.shape[2]
    norm_factor = 1.0 / math.sqrt(seq_dev * lax.axis_size("dp"))
    own_grad = jnp.where(core == 1, cotangent[1], cotangent[0])
    own_grad, saved_short, saved_medium = lax.optimization_barrier(
        (own_grad, saved_short, saved_medium)
    )
    gated = (saved_short[0].astype(jnp.float32) * saved_medium[0].astype(jnp.float32)).astype(
        jnp.bfloat16
    )
    in_part = jnp.dot(
        gated.reshape(micro_count * seq_dev, width), proj_in[0], preferred_element_type=jnp.float32
    )
    in_full = tensor_sum(in_part).reshape(micro_count, seq_dev, rank)
    in_kept = jnp.where(core == 1, in_full[1], in_full[0])
    in_got = swapped(jnp.where(core == 1, in_full[0], in_full[1]))
    in_low = jnp.where(core == 1, in_got, in_kept)
    in_high = jnp.where(core == 1, in_kept, in_got)

    basis = lax.dynamic_slice_in_dim(proj_out[0], shard * width, width, axis=0)
    basis_got = swapped(basis)
    basis_low = jnp.where(core == 1, basis_got, basis)
    basis_high = jnp.where(core == 1, basis, basis_got)

    def outer(in_side, out_part):
        return lax.dot_general(
            in_side, out_part, (((0,), (0,)), ((), ())), precision=lax.Precision.HIGHEST
        )

    part_high = outer(in_high, jnp.dot(own_grad, basis_high, preferred_element_type=jnp.float32))

    in_rim, saved_short, saved_medium, short_filter, medium_filter = lax.optimization_barrier(
        (
            with_rim_before(in_low, medium_filter.shape[1]),
            saved_short, saved_medium, short_filter, medium_filter,
        )
    )
    saved = jnp.stack([saved_short[0, 0], saved_medium[0, 0]])
    saved_got = lax.ppermute(saved, "pipe", [(1, 0)])
    short_act = jnp.where(core == 1, saved_short[0, 1], saved_got[0])
    medium_act = jnp.where(core == 1, saved_medium[0, 1], saved_got[1])
    taps = from_section(jnp.concatenate([short_filter[0], medium_filter[0]], axis=0), 1)
    short_count = short_filter.shape[1]
    short_taps, medium_taps = taps[:short_count], taps[short_count:]
    shifted = shifted_rows(in_rim, medium_taps.shape[0])
    direct = outer(in_low, own_grad.astype(jnp.float32))
    part_low = filtered_outer(
        back_parts(own_grad, out_weight[0], shard),
        short_act, medium_act, shifted, short_taps, medium_taps, direct, basis_low,
    )

    sums = sum_everywhere(jnp.stack([part_low, part_high])) * norm_factor
    kept = jnp.where(core == 1, sums[1], sums[0])
    got = swapped(jnp.where(core == 1, sums[0], sums[1]))
    return jnp.where(core == 1, jnp.stack([got, kept]), jnp.stack([kept, got]))[None]


def solution(mesh):
    in_specs = (
        P(None, "dp", "tensor"),
        P("pipe", None, "dp", "tensor"),
        P("pipe", None, "dp", "tensor"),
        P("pipe", "tensor", None),
        P("pipe", None, "tensor"),
        P("pipe", None, "tensor"),
        P("pipe", "tensor", None),
        P("pipe", None, None),
    )
    out_specs = P("pipe", None, None, None)
    return jax.shard_map(body, mesh=mesh, in_specs=in_specs, out_specs=out_specs, check_vma=False)
```
